128 devices in a mesh: tm: 32 (over z, y, core), row: 4 (over x).
Axes of the slice: x: 4, y: 4, z: 4, core: 2. Of those that a mesh axis runs over, the one named last changes fastest.
Arguments:
- edge_factor: float32 [32, 512, 512], P('tm', 'row'), may hold values from -0.25 to 0.25
- mass: float32 [32, 512], P('tm', 'row'), may hold values from 0.001 to 0.01
- rhs: float32 [32, 512, 512], P('tm', None, 'row'), may hold values from -0.25 to 0.25
Outputs:
- solution: float32 [32, 512, 512], P('tm', None, 'row')
The draws below stay inside these ranges and needn't reach their ends.
All inputs are finite; a program needn't handle non-finite values.
Results may differ from the reference program's by a relative error of at most 0.0003.
Values sent between devices are 32-bit elements; how exact they have to be, the bound alone decides.
A program may use at most 128 MiB of HBM per device.

```python
import math
import jax
import jax.numpy as jnp
from jax import lax

NODES = 512
BLOCKS = 32
RHS = 512


def draw_rhs(key, part):
    shape_all = (BLOCKS, NODES, RHS)
    return jnp.clip(0.05 * jax.random.normal(key, shape_all, jnp.float32), -0.25, 0.25)


def shard_levels(stream_key, extent, shards, smallest, top_value):
    loudness, own = 1.0, jax.random.fold_in(stream_key, 6)
    for position, shards_of in shards:
        steps = jnp.exp(jax.random.uniform(jax.random.fold_in(own, position), (shards_of,), jnp.float32, smallest / len(shards), top_value / len(shards)))
        loudness = loudness * jnp.repeat(steps, extent[position] // shards_of).reshape([-1 if axis == position else 1 for axis in range(len(extent))])
    return loudness


def noise(stream_key, extent, scale, most, cuts=(), held_as=jnp.bfloat16):
    values = jax.random.normal(stream_key, extent, jnp.float32) * scale
    if len(cuts) > 0:
        values = shard_levels(stream_key, extent, cuts, -0.22, 0.18) * values
    return jnp.clip(values, min=-most, max=most).astype(held_as)


def setup_inputs(seed: int = 0) -> dict:
    keys = jax.random.split(jax.random.key(seed), 4)
    edge_factor = noise(keys[0], (BLOCKS, NODES, NODES), NODES ** -0.5, 0.25, ((0, 32), (1, 4)), jnp.float32)
    mass = jnp.clip(jnp.exp(math.log(0.01) - 2.30258502 * jax.random.uniform(keys[1], (BLOCKS, NODES), jnp.float32) ** shard_levels(keys[1], (BLOCKS, NODES), ((0, 32), (1, 4)), -0.2, 0.2)), 0.001, 0.01)
    rhs = draw_rhs(jax.random.fold_in(keys[3], 71), 0)
    return {"edge_factor": edge_factor, "mass": mass, "rhs": rhs}


exact_prec = lax.Precision.HIGHEST

def edge_gram(factor):
    return jnp.dot(factor.astype(jnp.float32), factor.T.astype(jnp.float32), precision=exact_prec, preferred_element_type=jnp.float32)

def solve_lower(factor, values):
    return jax.scipy.linalg.solve_triangular(factor, values, lower=True)

def reference(edge_factor, mass, rhs):
    edge_all = lax.map(edge_gram, edge_factor)
    zero_block = jnp.zeros((1, NODES, NODES), jnp.float32)
    edge_next = jnp.concatenate([edge_all[1:], zero_block], axis=0)
    mass_diag = jax.vmap(jnp.diag)(mass)
    diag_blocks = mass_diag + edge_all + edge_next
    keep_mask = (jnp.arange(BLOCKS) > 0).astype(jnp.float32)[:, None, None]
    low_blocks = -edge_all * keep_mask
    low_next = jnp.concatenate([low_blocks[1:], zero_block], axis=0)

    def forward(state_pair, step_in):
        factor_prev, carried = state_pair
        diag_block, low_block, rhs_block = step_in
        whitened = solve_lower(factor_prev, low_block.T)
        schur_block = diag_block - jnp.dot(whitened.T, whitened, precision=exact_prec)
        carried_solve = solve_lower(factor_prev, carried)
        reduced = rhs_block - jnp.dot(whitened.T, carried_solve, precision=exact_prec)
        factor = jnp.linalg.cholesky(schur_block)
        return ((factor, reduced), (factor, reduced))
    start_pair = (jnp.eye(NODES, dtype=jnp.float32), jnp.zeros((NODES, RHS), jnp.float32))
    _, (factors, reduced_all) = lax.scan(forward, start_pair, (diag_blocks, low_blocks, rhs))

    def backward(next_solution, step_in):
        factor, reduced, low_after = step_in
        rhs_value = reduced - jnp.dot(low_after.T, next_solution, precision=exact_prec)
        inner = solve_lower(factor, rhs_value)
        current = jax.scipy.linalg.solve_triangular(factor, inner, lower=True, trans=1)
        return (current, current)
    _, solution = lax.scan(backward, jnp.zeros((NODES, RHS), jnp.float32), (factors, reduced_all, low_next), reverse=True)
    return solution
```

```python
import functools

import jax
import jax.numpy as jnp
from jax import lax
from jax.experimental import pallas as pl
from jax.experimental.pallas import tpu as pltpu
from jax.sharding import PartitionSpec as P

MESH = pl.DeviceIdType.MESH
EXACT = lax.Precision.HIGHEST
Q = 128
G = 8


def dot(a, b, ca=1, cb=0):
    return lax.dot_general(
        a, b, (((ca,), (cb,)), ((), ())), precision=EXACT, preferred_element_type=jnp.float32
    )


def lanes(v, k):
    return jnp.broadcast_to(v[:, k : k + 1], v.shape)


def subs(v, k):
    return jnp.broadcast_to(v[k : k + 1, :], v.shape)


def inverse_factor(rows):
    lane = lax.broadcasted_iota(jnp.int32, (G, Q), 1)
    sub = lax.broadcasted_iota(jnp.int32, (G, Q), 0)
    rows = list(rows)
    count = len(rows)
    out = []
    for g in range(count):
        c0 = G * g
        inside = (lane >= c0) & (lane < c0 + G)
        cols = [lanes(rows[g], c0 + k) for k in range(G)]
        v = jnp.where(inside, jnp.where(lane == sub + c0, 1.0, 0.0), rows[g])
        inv, upper = [], {}
        scale = jnp.ones((G, Q), jnp.float32)
        for k in range(G):
            pivot = subs(cols[k], k)
            inv.append(1.0 / pivot)
            scale = jnp.where(sub == k, lax.rsqrt(pivot), scale)
            if k < G - 1:
                m = jnp.where(sub > k, cols[k] * inv[k], 0.0)
                for k2 in range(k + 1, G):
                    upper[k, k2] = subs(cols[k2], k)
                    cols[k2] = cols[k2] - m * upper[k, k2]
                v = v - m * subs(v, k)
        spread = [subs(v, k) for k in range(G)]
        for h in range(g + 1, count):
            below = [lanes(rows[h], c0 + k) for k in range(G)]
            w = jnp.where(inside, 0.0, rows[h])
            for k in range(G):
                m = below[k] * inv[k]
                for k2 in range(k + 1, G):
                    below[k2] = below[k2] - m * upper[k, k2]
                w = w - m * spread[k]
            rows[h] = w
        out.append(jnp.where(lane <= sub + c0, v * scale, 0.0))
    return out


def side(blocks):
    return jnp.concatenate(blocks, axis=1)


def factorize(a, panel):
    tiles = a.shape[0]

    def step(j, carry):
        here = pl.ds(pl.multiple_of(j * Q, Q), Q)
        rows = [a[j, pl.ds(pl.multiple_of(j * Q + G * h, G), G), :] for h in range(Q // G)]
        top = jnp.concatenate(inverse_factor(rows), axis=0)
        across = dot(top, side([a[c, here, :] for c in range(tiles)]))
        for c in range(tiles):
            block = jnp.where(c == j, top, across[:, c * Q : (c + 1) * Q])
            panel[c] = block
            a[c, here, :] = jnp.where(c <= j, block, 0.0)
        for i in range(1, tiles):

            @pl.when(i > j)
            def _():
                there = slice(i * Q, (i + 1) * Q)
                update = dot(panel[i], side([panel[c] for c in range(tiles)]), 0, 0)
                for c in range(tiles):
                    old = jnp.where(c == j, 0.0, a[c, there, :])
                    a[c, there, :] = old - update[:, c * Q : (c + 1) * Q]

        return carry

    lax.fori_loop(0, tiles, step, 0)


def kernel(blocks, levels, f_ref, mass_ref, rhs_ref, out_ref, a, panel, w, rcur, fown, fnext, massg, dg, lg, ug, dr, rr, staged,
           fsend, frecv, nsend, nrecv, msend, mrecv, send, recv):
    t = lax.axis_index("tm")
    r = lax.axis_index("row")
    tiles = a.shape[0]

    def peer(d):
        return (t, lax.rem(r + d, tiles))

    def source(d):
        return lax.rem(r + tiles - d, tiles)

    def copy(src, dst, ssem, rsem, device):
        return pltpu.make_async_remote_copy(
            src_ref=src, dst_ref=dst, send_sem=ssem, recv_sem=rsem, device_id=device, device_id_type=MESH
        )

    barrier = pltpu.get_barrier_semaphore()
    expected = tiles - 1
    for d in range(1, tiles):
        pl.semaphore_signal(barrier, inc=1, device_id=peer(d), device_id_type=MESH)
    for level in range(levels):
        s = 2**level
        up, down = t + s < blocks, t >= s

        @pl.when(up)
        def _():
            pl.semaphore_signal(barrier, inc=1, device_id=(t + s, r), device_id_type=MESH)

        @pl.when(down)
        def _():
            pl.semaphore_signal(barrier, inc=1, device_id=(t - s, r), device_id_type=MESH)

        expected = expected + up.astype(jnp.int32) + down.astype(jnp.int32)
    pl.semaphore_wait(barrier, expected)

    def f_copy(d):
        return copy(f_ref, fown.at[r], fsend.at[d - 1], frecv.at[d - 1], peer(d))

    def f_arrived(d):
        return copy(f_ref, fown.at[source(d)], fsend.at[d - 1], frecv.at[d - 1], peer(d))

    def m_copy(d):
        return copy(mass_ref, massg.at[r], msend.at[d - 1], mrecv.at[d - 1], peer(d))

    def m_arrived(d):
        return copy(mass_ref, massg.at[source(d)], msend.at[d - 1], mrecv.at[d - 1], peer(d))

    def n_copy(d):
        src = f_ref if d == 0 else fown.at[source(d)]
        return copy(src, fnext.at[source(d)], nsend.at[d], nrecv.at[d], (t - 1, r))

    order = (1, 3, 2)
    for d in order:
        f_copy(d).start()
    for d in order:
        m_copy(d).start()

    @pl.when(t >= 1)
    def _():
        n_copy(0).start()

    fown[r] = f_ref[...]
    massg[r] = mass_ref[...]
    rcur[...] = rhs_ref[...]
    for d in order:
        f_arrived(d).wait_recv()

        @pl.when(t >= 1)
        def _():
            n_copy(d).start()

    for d in order:
        m_arrived(d).wait_recv()

    row_ids = lax.broadcasted_iota(jnp.int32, (tiles * Q, Q), 0)
    col_ids = lax.broadcasted_iota(jnp.int32, (tiles * Q, Q), 1)

    def own_gram(p, carry):
        full = fown[...].reshape(tiles * Q, tiles * Q)
        pair = fown[pl.ds(2 * p, 2)].reshape(2 * Q, tiles * Q)
        gram = dot(full, pair, 1, 1)
        for e in range(2):
            c = 2 * p + e
            block = gram[:, e * Q : (e + 1) * Q]
            lg[0, c] = -block
            dg[0, c] = block + jnp.where(row_ids == col_ids + c * Q, massg[c], 0.0)
        return carry

    lax.fori_loop(0, tiles // 2, own_gram, 0)

    @pl.when(t + 1 < blocks)
    def _():
        for d in (0,) + order:
            n_copy(d).wait_recv()

        def next_gram(p, carry):
            full = fnext[...].reshape(tiles * Q, tiles * Q)
            pair = fnext[pl.ds(2 * p, 2)].reshape(2 * Q, tiles * Q)
            gram = dot(full, pair, 1, 1)
            for e in range(2):
                c = 2 * p + e
                block = gram[:, e * Q : (e + 1) * Q]
                ug[0, c] = -block
                dg[0, c] = dg[0, c] + block
            return carry

        lax.fori_loop(0, tiles // 2, next_gram, 0)

    for d in order:
        f_copy(d).wait_send()
        m_copy(d).wait_send()

    @pl.when(t >= 1)
    def _():
        for d in (0,) + order:
            n_copy(d).wait_send()

    def along(i, s, k):
        device = (t + s, r) if k % 2 == 0 else (t - s, r)
        target = {0: dr, 1: dr, 4: rr, 5: rr}.get(k)
        if target is not None:
            dst = target.at[i, k % 2]
        else:
            dst = (lg if k == 2 else ug).at[i + 1, r]
        return copy(staged.at[i, k], dst, send.at[i, k], recv.at[i, k], device)

    def across_row(i, k, d, slot):
        buffer = (dg, lg, ug)[k]
        sem = 6 + 3 * k + d - 1
        return copy(buffer.at[i + 1, r], buffer.at[i + 1, slot], send.at[i, sem], recv.at[i, sem], peer(d))

    def take_rhs(i, s):
        @pl.when(t >= s)
        def _():
            along(i, s, 4).wait_recv()
            rcur[...] = rcur[...] - rr[i, 0]

        @pl.when(t + s < blocks)
        def _():
            along(i, s, 5).wait_recv()
            rcur[...] = rcur[...] - rr[i, 1]

    def gather_arrived(i, k):
        for d in order:
            across_row(i, k, d, source(d)).wait_recv()

    def whiten(src, i, base):
        def pair(p, carry):
            inverse = side([a[c] for c in range(tiles)])
            both = dot(inverse, side([src[i, 2 * p], src[i, 2 * p + 1]]))
            w[base + 2 * p] = both[:, :Q]
            w[base + 2 * p + 1] = both[:, Q:]
            return carry

        lax.fori_loop(0, tiles // 2, pair, 0)

    def level(i, s):
        up, down = t + s < blocks, t >= s
        for c in range(tiles):
            a[c] = dg[i, c]
        factorize(a, panel)

        @pl.when(i > 0)
        def _():
            take_rhs(i - 1, s // 2)

        @pl.when(down & (i > 0))
        def _():
            gather_arrived(i - 1, 1)

        @pl.when(up & (i > 0))
        def _():
            gather_arrived(i - 1, 2)

        @pl.when(up)
        def _():
            whiten(ug, i, tiles)
            later = side([w[tiles + c] for c in range(tiles)])
            staged[i, 0] = dot(later, w[tiles + r], 0, 0)
            along(i, s, 0).start()

        @pl.when(down)
        def _():
            whiten(lg, i, 0)
            earlier = side([w[c] for c in range(tiles)])
            staged[i, 1] = dot(earlier, w[r], 0, 0)
            along(i, s, 1).start()

        @pl.when(up & down)
        def _():
            later = side([w[tiles + c] for c in range(tiles)])
            staged[i, 2] = -dot(later, w[r], 0, 0)
            along(i, s, 2).start()
            earlier = side([w[c] for c in range(tiles)])
            staged[i, 3] = -dot(earlier, w[tiles + r], 0, 0)
            along(i, s, 3).start()

        w[2 * tiles] = dot(side([a[c] for c in range(tiles)]), rcur[...])

        @pl.when(up)
        def _():
            later = side([w[tiles + c] for c in range(tiles)])
            staged[i, 4] = dot(later, w[2 * tiles], 0, 0)
            along(i, s, 4).start()

        @pl.when(down)
        def _():
            earlier = side([w[c] for c in range(tiles)])
            staged[i, 5] = dot(earlier, w[2 * tiles], 0, 0)
            along(i, s, 5).start()

        @pl.when(i < levels)
        def _():
            dg[i + 1, r] = dg[i, r]

            @pl.when(down)
            def _():
                along(i, s, 0).wait_recv()
                dg[i + 1, r] = dg[i + 1, r] - dr[i, 0]

            @pl.when(up)
            def _():
                along(i, s, 1).wait_recv()
                dg[i + 1, r] = dg[i + 1, r] - dr[i, 1]

            for d in order:
                across_row(i, 0, d, r).start()

            @pl.when(t >= 2 * s)
            def _():
                along(i, s, 2).wait_recv()
                for d in order:
                    across_row(i, 1, d, r).start()

            @pl.when(t + 2 * s < blocks)
            def _():
                along(i, s, 3).wait_recv()
                for d in order:
                    across_row(i, 2, d, r).start()

            gather_arrived(i, 0)

        return s * 2

    lax.fori_loop(0, levels + 1, level, 1)
    out_ref[...] = dot(side([a[c] for c in range(tiles)]), w[2 * tiles], 0, 0)

    def drain(i, s):
        up, down = t + s < blocks, t >= s

        @pl.when(up)
        def _():
            along(i, s, 0).wait_send()
            along(i, s, 4).wait_send()

        @pl.when(down)
        def _():
            along(i, s, 1).wait_send()
            along(i, s, 5).wait_send()

        @pl.when(up & down)
        def _():
            along(i, s, 2).wait_send()
            along(i, s, 3).wait_send()

        for d in order:
            across_row(i, 0, d, r).wait_send()

        @pl.when(t >= 2 * s)
        def _():
            for d in order:
                across_row(i, 1, d, r).wait_send()

        @pl.when(t + 2 * s < blocks)
        def _():
            for d in order:
                across_row(i, 2, d, r).wait_send()

        return s * 2

    lax.fori_loop(0, levels, drain, 1)


def local(edge_factor, mass, rhs):
    blocks = lax.axis_size("tm")
    tiles = lax.axis_size("row")
    levels = (blocks - 1).bit_length()
    quarter, nodes = edge_factor.shape[1:]
    f32 = jnp.float32
    vmem = pl.BlockSpec(memory_space=pltpu.VMEM)
    dma = pltpu.SemaphoreType.DMA
    column = (nodes, quarter)
    mass_rows = jnp.broadcast_to(mass, (1, quarter))
    result = pl.pallas_call(
        functools.partial(kernel, blocks, levels),
        out_shape=jax.ShapeDtypeStruct(column, f32),
        in_specs=[vmem] * 3,
        out_specs=vmem,
        scratch_shapes=[
            pltpu.VMEM((tiles,) + column, f32),
            pltpu.VMEM((tiles, quarter, quarter), f32),
            pltpu.VMEM((2 * tiles + 1,) + column, f32),
            pltpu.VMEM(column, f32),
            pltpu.VMEM((tiles, quarter, nodes), f32),
            pltpu.VMEM((tiles, quarter, nodes), f32),
            pltpu.VMEM((tiles, 1, quarter), f32),
            pltpu.VMEM((levels + 1, tiles) + column, f32),
            pltpu.VMEM((levels + 1, tiles) + column, f32),
            pltpu.VMEM((levels + 1, tiles) + column, f32),
            pltpu.VMEM((levels, 2) + column, f32),
            pltpu.VMEM((levels, 2) + column, f32),
            pltpu.VMEM((levels, 6) + column, f32),
            dma((3,)), dma((3,)), dma((4,)), dma((4,)), dma((3,)), dma((3,)),
            dma((levels, 15)), dma((levels, 15)),
        ],
        compiler_params=pltpu.CompilerParams(
            collective_id=0, has_side_effects=True, vmem_limit_bytes=63 * 1024 * 1024
        ),
    )(edge_factor[0], mass_rows, rhs[0])
    return result[None]


def solution(mesh):
    placed = (P("tm", "row", None), P("tm", "row"), P("tm", None, "row"))
    return jax.shard_map(
        local, mesh=mesh, in_specs=placed, out_specs=P("tm", None, "row"), check_vma=False
    )
```

```python
import functools

import jax
import jax.numpy as jnp
from jax import lax
from jax.experimental import pallas as pl
from jax.experimental.pallas import tpu as pltpu
from jax.sharding import PartitionSpec as P

MESH = pl.DeviceIdType.MESH
EXACT = lax.Precision.HIGHEST
Q = 128
SPREAD = (0, 1)
G = 8


def dot(a, b, ca=1, cb=0):
    return lax.dot_general(
        a, b, (((ca,), (cb,)), ((), ())), precision=EXACT, preferred_element_type=jnp.float32
    )


def lanes(v, k):
    return jnp.broadcast_to(v[:, k : k + 1], v.shape)


def subs(v, k):
    return jnp.broadcast_to(v[k : k + 1, :], v.shape)


def eliminate(rows, base):
    lane = lax.broadcasted_iota(jnp.int32, (G, Q), 1)
    sub = lax.broadcasted_iota(jnp.int32, (G, Q), 0)
    rows = list(rows)
    count = len(rows)
    out = []
    cols = [lanes(rows[0], base + k) for k in range(G)]
    for g in range(count):
        c0 = base + G * g
        inside = (lane >= c0) & (lane < c0 + G)
        more = g + 1 < count
        if more:
            near = [lanes(rows[g + 1], c0 + k) for k in range(G)]
            after = [lanes(rows[g + 1], c0 + G + k) for k in range(G)]
            w = jnp.where(inside, 0.0, rows[g + 1])
        v = jnp.where(inside, jnp.where(lane == sub + c0, 1.0, 0.0), rows[g])
        inv, upper = [], {}
        scale = jnp.ones((G, Q), jnp.float32)
        for k in range(G):
            pivot = subs(cols[k], k)
            inv.append(1.0 / pivot)
            scale = jnp.where(sub == k, lax.rsqrt(pivot), scale)
            for k2 in range(k + 1, G):
                upper[k, k2] = subs(cols[k2], k)
            row = subs(v, k)
            if k < G - 1:
                m = jnp.where(sub > k, cols[k] * inv[k], 0.0)
                for k2 in range(k + 1, G):
                    cols[k2] = cols[k2] - m * upper[k, k2]
                v = v - m * row
            if more:
                m = near[k] * inv[k]
                for k2 in range(G):
                    after[k2] = after[k2] - m * subs(near[k], k2)
                for k2 in range(k + 1, G):
                    near[k2] = near[k2] - m * upper[k, k2]
                w = w - m * row
        if more:
            rows[g + 1] = w
            cols = after
        spread = [subs(v, k) for k in range(G)]
        for h in range(g + 2, count):
            below = [lanes(rows[h], c0 + k) for k in range(G)]
            w = jnp.where(inside, 0.0, rows[h])
            for k in range(G):
                m = below[k] * inv[k]
                for k2 in range(k + 1, G):
                    below[k2] = below[k2] - m * upper[k, k2]
                w = w - m * spread[k]
            rows[h] = w
        out.append(v * scale)
    return out


def inverse_factor(rows):
    lane = lax.broadcasted_iota(jnp.int32, (G, Q), 1)
    sub = lax.broadcasted_iota(jnp.int32, (G, Q), 0)
    half, middle = len(rows) // 2, Q // 2
    top = eliminate(rows[:half], 0)
    kept = [jnp.where((lane <= sub + G * g) | (lane >= middle), top[g], 0.0) for g in range(half)]
    stacked = jnp.concatenate(kept, axis=0)
    update = dot(stacked, stacked, 0, 0)
    rest = [jnp.where(lane < middle, 0.0, rows[h]) - update[G * h : G * h + G] for h in range(half, 2 * half)]
    both = top + eliminate(rest, middle)
    return [jnp.where(lane <= sub + G * g, both[g], 0.0) for g in range(2 * half)]


def side(blocks):
    return jnp.concatenate(blocks, axis=1)


def factorize(diag, inverse, upper, before, after):
    tiles = diag.shape[0]

    def step(j, carry):
        here = pl.ds(pl.multiple_of(j * Q, Q), Q)
        before(j)
        for c in range(tiles):
            inverse[c, here, :] = jnp.where(c < j, 0.0, diag[c, here, :])
        for above in range(1, tiles):

            @pl.when(j == above)
            def _():
                rows = slice(0, above * Q)
                known = [(inverse if c < above else upper)[c, rows, :] for c in range(tiles)]
                update = dot(upper[above, rows, :], side(known), 0, 0)
                for c in range(tiles):
                    inverse[c, here, :] = inverse[c, here, :] - update[:, c * Q : (c + 1) * Q]

        rows = [inverse[j, pl.ds(pl.multiple_of(j * Q + G * h, G), G), :] for h in range(Q // G)]
        top = jnp.concatenate(inverse_factor(rows), axis=0)
        across = dot(top, side([inverse[c, here, :] for c in range(tiles)]))
        for c in range(tiles):
            block = across[:, c * Q : (c + 1) * Q]
            upper[c, here, :] = block
            inverse[c, here, :] = jnp.where(c == j, top, jnp.where(c < j, block, 0.0))
        after(j)
        return carry

    lax.fori_loop(0, tiles, step, 0)


def kernel(blocks, levels, f_ref, mass_ref, rhs_ref, out_ref, a, upper, w, rcur, fown, fnext, massg, dg, lg, ug, dr, rr, staged, pairs,
           fsend, frecv, nsend, nrecv, msend, mrecv, send, recv):
    t = lax.axis_index("tm")
    r = lax.axis_index("row")
    tiles = a.shape[0]

    def peer(d):
        return (t, lax.rem(r + d, tiles))

    def source(d):
        return lax.rem(r + tiles - d, tiles)

    def copy(src, dst, ssem, rsem, device):
        return pltpu.make_async_remote_copy(
            src_ref=src, dst_ref=dst, send_sem=ssem, recv_sem=rsem, device_id=device, device_id_type=MESH
        )

    barrier = pltpu.get_barrier_semaphore()
    expected = tiles - 1
    for d in range(1, tiles):
        pl.semaphore_signal(barrier, inc=1, device_id=peer(d), device_id_type=MESH)
    for level in range(levels):
        s = 2**level
        up, down = t + s < blocks, t >= s

        @pl.when(up)
        def _():
            pl.semaphore_signal(barrier, inc=1, device_id=(t + s, r), device_id_type=MESH)

        @pl.when(down)
        def _():
            pl.semaphore_signal(barrier, inc=1, device_id=(t - s, r), device_id_type=MESH)

        expected = expected + up.astype(jnp.int32) + down.astype(jnp.int32)
    pl.semaphore_wait(barrier, expected)

    def f_copy(d):
        return copy(f_ref, fown.at[r], fsend.at[d - 1], frecv.at[d - 1], peer(d))

    def f_arrived(d):
        return copy(f_ref, fown.at[source(d)], fsend.at[d - 1], frecv.at[d - 1], peer(d))

    def f_on(d, slot):
        half = pl.ds(0 if d == 1 else Q // 2, Q // 2)
        sem = 1 if d == 1 else 3
        return copy(fown.at[slot, half], fown.at[slot, half], fsend.at[sem], frecv.at[sem], peer(d))

    def m_copy(d):
        return copy(mass_ref, massg.at[r], msend.at[d - 1], mrecv.at[d - 1], peer(d))

    def m_arrived(d):
        return copy(mass_ref, massg.at[source(d)], msend.at[d - 1], mrecv.at[d - 1], peer(d))

    def n_copy(d):
        src = f_ref if d == 0 else fown.at[source(d)]
        return copy(src, fnext.at[source(d)], nsend.at[d], nrecv.at[d], (t - 1, r))

    order = (1, 3, 2)
    for d in (1, 3):
        f_copy(d).start()
    for d in order:
        m_copy(d).start()

    @pl.when(t >= 1)
    def _():
        n_copy(0).start()

    fown[r] = f_ref[...]
    massg[r] = mass_ref[...]
    rcur[...] = rhs_ref[...]
    for d in (1, 3):
        f_arrived(d).wait_recv()
        f_on(d, source(d)).start()

        @pl.when(t >= 1)
        def _():
            n_copy(d).start()

    for d in (1, 3):
        f_on(d, source(2)).wait_recv()

    @pl.when(t >= 1)
    def _():
        n_copy(2).start()

    for d in order:
        m_arrived(d).wait_recv()

    row_ids = lax.broadcasted_iota(jnp.int32, (tiles * Q, Q), 0)
    col_ids = lax.broadcasted_iota(jnp.int32, (tiles * Q, Q), 1)

    def own_gram(p, carry):
        full = fown[...].reshape(tiles * Q, tiles * Q)
        pair = fown[pl.ds(2 * p, 2)].reshape(2 * Q, tiles * Q)
        gram = dot(full, pair, 1, 1)
        for e in range(2):
            c = 2 * p + e
            block = gram[:, e * Q : (e + 1) * Q]
            lg[0, c] = -block
            dg[0, c] = block + jnp.where(row_ids == col_ids + c * Q, massg[c], 0.0)
        return carry

    lax.fori_loop(0, tiles // 2, own_gram, 0)

    @pl.when(t + 1 < blocks)
    def _():
        for d in (0,) + order:
            n_copy(d).wait_recv()

        def next_gram(p, carry):
            full = fnext[...].reshape(tiles * Q, tiles * Q)
            pair = fnext[pl.ds(2 * p, 2)].reshape(2 * Q, tiles * Q)
            gram = dot(full, pair, 1, 1)
            for e in range(2):
                c = 2 * p + e
                block = gram[:, e * Q : (e + 1) * Q]
                ug[0, c] = -block
                dg[0, c] = dg[0, c] + block
            return carry

        lax.fori_loop(0, tiles // 2, next_gram, 0)

    for d in (1, 3):
        f_copy(d).wait_send()
        f_on(d, source(d)).wait_send()
    for d in order:
        m_copy(d).wait_send()

    @pl.when(t >= 1)
    def _():
        for d in (0,) + order:
            n_copy(d).wait_send()

    def along(i, s, k, c=None):
        device = (t + s, r) if k % 2 == 0 else (t - s, r)
        if k < 2:
            rows = pl.ds(c * Q, Q)
            src, dst, sem = staged.at[i, k, rows], dr.at[i, k, rows], 4 * k + c
        elif k < 4:
            src, dst, sem = pairs.at[i, k - 2, c], (lg if k == 2 else ug).at[i + 1, lax.rem(r + c, tiles)], 6 + 2 * k + c
        else:
            src, dst, sem = staged.at[i, k - 2], rr.at[i, k % 2], 10 + k
        return copy(src, dst, send.at[i, sem], recv.at[i, sem], device)

    def rows_across(i, c, d, slot):
        rows = pl.ds(c * Q, Q)
        sem = 16 + 3 * c + d - 1
        return copy(dg.at[i + 1, r, rows], dg.at[i + 1, slot, rows], send.at[i, sem], recv.at[i, sem], peer(d))

    def coupling_across(i, k, d):
        buffer = (lg, ug)[k]
        slot = r if d == 1 else lax.rem(r + 1, tiles)
        sem = 28 + 2 * k + (0 if d == 1 else 1)
        return copy(buffer.at[i + 1, slot], buffer.at[i + 1, slot], send.at[i, sem], recv.at[i, sem], peer(d))

    def coupling_arrives(i, k, d):
        buffer = (lg, ug)[k]
        slot = lax.rem(r + (3 if d == 1 else 2), tiles)
        sem = 28 + 2 * k + (0 if d == 1 else 1)
        return copy(buffer.at[i + 1, slot], buffer.at[i + 1, slot], send.at[i, sem], recv.at[i, sem], peer(d))

    def couples(i, s, k):
        return (t >= 2 * s) if k == 0 else (t + 2 * s < blocks)

    def take_rows(i, s, c):
        rows = slice(c * Q, (c + 1) * Q)
        dg[i + 1, r, rows] = dg[i, r, rows]

        @pl.when(t >= s)
        def _():
            along(i, s, 0, c).wait_recv()
            dg[i + 1, r, rows] = dg[i + 1, r, rows] - dr[i, 0, rows]

        @pl.when(t + s < blocks)
        def _():
            along(i, s, 1, c).wait_recv()
            dg[i + 1, r, rows] = dg[i + 1, r, rows] - dr[i, 1, rows]

        for d in order:
            rows_across(i, c, d, r).start()

    def spread_couplings(i, s, k):
        @pl.when(couples(i, s, k))
        def _():
            for c in range(2):
                along(i, s, 2 + k, c).wait_recv()
            for d in (1, 3):
                coupling_across(i, k, d).start()

    def couplings_arrived(i, s, k):
        @pl.when(couples(i, s, k))
        def _():
            for d in (1, 3):
                coupling_arrives(i, k, d).wait_recv()

    def take_rhs(i, s):
        @pl.when(t >= s)
        def _():
            along(i, s, 4).wait_recv()
            rcur[...] = rcur[...] - rr[i, 0]

        @pl.when(t + s < blocks)
        def _():
            along(i, s, 5).wait_recv()
            rcur[...] = rcur[...] - rr[i, 1]

    def under(values):
        half = tiles // 2
        cut = half * Q
        upper_half = dot(side([a[c, :cut, :] for c in range(half)]), values[:cut])
        lower_half = dot(side([a[c, cut:, :] for c in range(tiles)]), values)
        return jnp.concatenate([upper_half, lower_half], axis=0)

    def whiten(src, i, base, p):
        first, second = lax.rem(r + 2 * p, tiles), lax.rem(r + 2 * p + 1, tiles)
        both = under(side([src[i, first], src[i, second]]))
        w[base + first] = both[:, :Q]
        w[base + second] = both[:, Q:]

    def level(i, s):
        up, down = t + s < blocks, t >= s
        past, reach = i - 1, s // 2

        def before(j):
            @pl.when(i > 0)
            def _():
                @pl.when(j == 0)
                def _():
                    take_rows(past, reach, 0)
                    take_rows(past, reach, 1)

                for d in order:
                    for c in range(tiles):

                        @pl.when(j == c)
                        def _():
                            rows_across(past, c, d, source(d)).wait_recv()

        def after(j):
            @pl.when(i > 0)
            def _():
                @pl.when(j == 0)
                def _():
                    take_rows(past, reach, 2)
                    take_rows(past, reach, 3)

                for k in range(2):

                    @pl.when(j == SPREAD[k])
                    def _():
                        spread_couplings(past, reach, k)

        factorize(dg.at[i], a, upper, before, after)

        @pl.when(up)
        def _():
            whiten(ug, i, tiles, 0)

        @pl.when(down)
        def _():
            whiten(lg, i, 0, 0)

        @pl.when(i > 0)
        def _():
            take_rhs(past, reach)

        w[2 * tiles] = under(rcur[...])

        @pl.when(i > 0)
        def _():
            couplings_arrived(past, reach, 0)
            couplings_arrived(past, reach, 1)

        @pl.when(up)
        def _():
            whiten(ug, i, tiles, 1)
            later = side([w[tiles + c] for c in range(tiles)])
            terms = dot(later, side([w[tiles + r], w[2 * tiles]]), 0, 0)
            staged[i, 0] = terms[:, :Q]
            staged[i, 2] = terms[:, Q:]
            for c in range(tiles):
                along(i, s, 0, c).start()

        @pl.when(down)
        def _():
            whiten(lg, i, 0, 1)
            earlier = side([w[c] for c in range(tiles)])
            terms = dot(earlier, side([w[r], w[2 * tiles]]), 0, 0)
            staged[i, 1] = terms[:, :Q]
            staged[i, 3] = terms[:, Q:]
            for c in range(tiles):
                along(i, s, 1, c).start()

        @pl.when(up & down)
        def _():
            second = lax.rem(r + 1, tiles)
            later = side([w[tiles + c] for c in range(tiles)])
            product = -dot(later, side([w[r], w[second]]), 0, 0)
            for c in range(2):
                pairs[i, 0, c] = product[:, c * Q : (c + 1) * Q]
                along(i, s, 2, c).start()
            earlier = side([w[c] for c in range(tiles)])
            product = -dot(earlier, side([w[tiles + r], w[tiles + second]]), 0, 0)
            for c in range(2):
                pairs[i, 1, c] = product[:, c * Q : (c + 1) * Q]
                along(i, s, 3, c).start()

        @pl.when(up)
        def _():
            along(i, s, 4).start()

        @pl.when(down)
        def _():
            along(i, s, 5).start()

        return s * 2

    lax.fori_loop(0, levels + 1, level, 1)
    out_ref[...] = dot(side([a[c] for c in range(tiles)]), w[2 * tiles], 0, 0)

    def drain(i, s):
        up, down = t + s < blocks, t >= s

        @pl.when(up)
        def _():
            for c in range(tiles):
                along(i, s, 0, c).wait_send()
            along(i, s, 4).wait_send()

        @pl.when(down)
        def _():
            for c in range(tiles):
                along(i, s, 1, c).wait_send()
            along(i, s, 5).wait_send()

        @pl.when(up & down)
        def _():
            for c in range(2):
                along(i, s, 2, c).wait_send()
                along(i, s, 3, c).wait_send()

        for c in range(tiles):
            for d in order:
                rows_across(i, c, d, r).wait_send()
        for k in range(2):

            @pl.when(couples(i, s, k))
            def _():
                for d in (1, 3):
                    coupling_across(i, k, d).wait_send()

        return s * 2

    lax.fori_loop(0, levels, drain, 1)


def local(edge_factor, mass, rhs):
    blocks = lax.axis_size("tm")
    tiles = lax.axis_size("row")
    levels = (blocks - 1).bit_length()
    quarter, nodes = edge_factor.shape[1:]
    f32 = jnp.float32
    vmem = pl.BlockSpec(memory_space=pltpu.VMEM)
    dma = pltpu.SemaphoreType.DMA
    column = (nodes, quarter)
    mass_rows = jnp.broadcast_to(mass, (1, quarter))
    result = pl.pallas_call(
        functools.partial(kernel, blocks, levels),
        out_shape=jax.ShapeDtypeStruct(column, f32),
        in_specs=[vmem] * 3,
        out_specs=vmem,
        scratch_shapes=[
            pltpu.VMEM((tiles,) + column, f32),
            pltpu.VMEM((tiles,) + column, f32),
            pltpu.VMEM((2 * tiles + 1,) + column, f32),
            pltpu.VMEM(column, f32),
            pltpu.VMEM((tiles, quarter, nodes), f32),
            pltpu.VMEM((tiles, quarter, nodes), f32),
            pltpu.VMEM((tiles, 1, quarter), f32),
            pltpu.VMEM((levels + 1, tiles) + column, f32),
            pltpu.VMEM((levels + 1, tiles) + column, f32),
            pltpu.VMEM((levels + 1, tiles) + column, f32),
            pltpu.VMEM((levels, 2) + column, f32),
            pltpu.VMEM((levels, 2) + column, f32),
            pltpu.VMEM((levels, 4) + column, f32),
            pltpu.VMEM((levels, 2, 2) + column, f32),
            dma((4,)), dma((4,)), dma((4,)), dma((4,)), dma((3,)), dma((3,)),
            dma((levels, 32)), dma((levels, 32)),
        ],
        compiler_params=pltpu.CompilerParams(
            collective_id=0, has_side_effects=True, vmem_limit_bytes=63 * 1024 * 1024
        ),
    )(edge_factor[0], mass_rows, rhs[0])
    return result[None]


def solution(mesh):
    placed = (P("tm", "row", None), P("tm", "row"), P("tm", None, "row"))
    return jax.shard_map(
        local, mesh=mesh, in_specs=placed, out_specs=P("tm", None, "row"), check_vma=False
    )
```

```python
import functools

import jax
import jax.numpy as jnp
from jax import lax
from jax.experimental import pallas as pl
from jax.experimental.pallas import tpu as pltpu
from jax.sharding import PartitionSpec as P

MESH = pl.DeviceIdType.MESH
EXACT = lax.Precision.HIGHEST
Q = 128
SPREAD = (1, 2)
G = 8


def dot(a, b, ca=1, cb=0):
    return lax.dot_general(
        a, b, (((ca,), (cb,)), ((), ())), precision=EXACT, preferred_element_type=jnp.float32
    )


def lanes(v, k):
    return jnp.broadcast_to(v[:, k : k + 1], v.shape)


def subs(v, k):
    return jnp.broadcast_to(v[k : k + 1, :], v.shape)


def eliminate(rows, base):
    lane = lax.broadcasted_iota(jnp.int32, (G, Q), 1)
    sub = lax.broadcasted_iota(jnp.int32, (G, Q), 0)
    rows = list(rows)
    count = len(rows)
    out = []
    cols = [lanes(rows[0], base + k) for k in range(G)]
    for g in range(count):
        c0 = base + G * g
        inside = (lane >= c0) & (lane < c0 + G)
        more = g + 1 < count
        if more:
            near = [lanes(rows[g + 1], c0 + k) for k in range(G)]
            after = [lanes(rows[g + 1], c0 + G + k) for k in range(G)]
            w = jnp.where(inside, 0.0, rows[g + 1])
        v = jnp.where(inside, jnp.where(lane == sub + c0, 1.0, 0.0), rows[g])
        inv, upper = [], {}
        scale = jnp.ones((G, Q), jnp.float32)
        for k in range(G):
            pivot = subs(cols[k], k)
            inv.append(1.0 / pivot)
            scale = jnp.where(sub == k, lax.rsqrt(pivot), scale)
            for k2 in range(k + 1, G):
                upper[k, k2] = subs(cols[k2], k)
            row = subs(v, k)
            if k < G - 1:
                m = jnp.where(sub > k, cols[k] * inv[k], 0.0)
                for k2 in range(k + 1, G):
                    cols[k2] = cols[k2] - m * upper[k, k2]
                v = v - m * row
            if more:
                m = near[k] * inv[k]
                for k2 in range(G):
                    after[k2] = after[k2] - m * subs(near[k], k2)
                for k2 in range(k + 1, G):
                    near[k2] = near[k2] - m * upper[k, k2]
                w = w - m * row
        if more:
            rows[g + 1] = w
            cols = after
        spread = [subs(v, k) for k in range(G)]
        for h in range(g + 2, count):
            below = [lanes(rows[h], c0 + k) for k in range(G)]
            w = jnp.where(inside, 0.0, rows[h])
            for k in range(G):
                m = below[k] * inv[k]
                for k2 in range(k + 1, G):
                    below[k2] = below[k2] - m * upper[k, k2]
                w = w - m * spread[k]
            rows[h] = w
        out.append(v * scale)
    return out


def inverse_factor(rows):
    lane = lax.broadcasted_iota(jnp.int32, (G, Q), 1)
    sub = lax.broadcasted_iota(jnp.int32, (G, Q), 0)
    half, middle = len(rows) // 2, Q // 2
    top = eliminate(rows[:half], 0)
    kept = [jnp.where((lane <= sub + G * g) | (lane >= middle), top[g], 0.0) for g in range(half)]
    stacked = jnp.concatenate(kept, axis=0)
    update = dot(stacked, stacked, 0, 0)
    rest = [jnp.where(lane < middle, 0.0, rows[h]) - update[G * h : G * h + G] for h in range(half, 2 * half)]
    both = top + eliminate(rest, middle)
    return [jnp.where(lane <= sub + G * g, both[g], 0.0) for g in range(2 * half)]


def side(blocks):
    return jnp.concatenate(blocks, axis=1)


def factorize(diag, inverse, upper, before, after):
    tiles = diag.shape[0]

    def step(j, carry):
        here = pl.ds(pl.multiple_of(j * Q, Q), Q)
        before(j)
        for c in range(tiles):
            inverse[c, here, :] = jnp.where(c < j, 0.0, diag[c, here, :])
        for above in range(1, tiles):

            @pl.when(j == above)
            def _():
                rows = slice(0, above * Q)
                known = [(inverse if c < above else upper)[c, rows, :] for c in range(tiles)]
                update = dot(upper[above, rows, :], side(known), 0, 0)
                for c in range(tiles):
                    inverse[c, here, :] = inverse[c, here, :] - update[:, c * Q : (c + 1) * Q]

        rows = [inverse[j, pl.ds(pl.multiple_of(j * Q + G * h, G), G), :] for h in range(Q // G)]
        top = jnp.concatenate(inverse_factor(rows), axis=0)
        across = dot(top, side([inverse[c, here, :] for c in range(tiles)]))
        for c in range(tiles):
            block = across[:, c * Q : (c + 1) * Q]
            upper[c, here, :] = block
            inverse[c, here, :] = jnp.where(c == j, top, jnp.where(c < j, block, 0.0))
        after(j)
        return carry

    lax.fori_loop(0, tiles, step, 0)


def kernel(blocks, levels, f_ref, mass_ref, rhs_ref, out_ref, a, upper, w, rcur, fown, fnext, massg, dg, lg, ug, dr, rr, staged, pairs,
           fsend, frecv, nsend, nrecv, msend, mrecv, send, recv):
    t = lax.axis_index("tm")
    r = lax.axis_index("row")
    tiles = a.shape[0]

    def peer(d):
        return (t, lax.rem(r + d, tiles))

    def source(d):
        return lax.rem(r + tiles - d, tiles)

    def copy(src, dst, ssem, rsem, device):
        return pltpu.make_async_remote_copy(
            src_ref=src, dst_ref=dst, send_sem=ssem, recv_sem=rsem, device_id=device, device_id_type=MESH
        )

    barrier = pltpu.get_barrier_semaphore()
    expected = tiles - 1
    for d in range(1, tiles):
        pl.semaphore_signal(barrier, inc=1, device_id=peer(d), device_id_type=MESH)
    for level in range(levels):
        s = 2**level
        up, down = t + s < blocks, t >= s

        @pl.when(up)
        def _():
            pl.semaphore_signal(barrier, inc=1, device_id=(t + s, r), device_id_type=MESH)

        @pl.when(down)
        def _():
            pl.semaphore_signal(barrier, inc=1, device_id=(t - s, r), device_id_type=MESH)

        expected = expected + up.astype(jnp.int32) + down.astype(jnp.int32)
    pl.semaphore_wait(barrier, expected)

    def half(h):
        return pl.ds(h * (Q // 2), Q // 2)

    def f_copy(d, h):
        sem = d - 1 + h
        return copy(f_ref.at[half(h)], fown.at[r, half(h)], fsend.at[sem], frecv.at[sem], peer(d))

    def f_arrived(d, h):
        sem = d - 1 + h
        return copy(f_ref.at[half(h)], fown.at[source(d), half(h)], fsend.at[sem], frecv.at[sem], peer(d))

    def f_on(d, slot):
        h = 0 if d == 1 else 1
        return copy(fown.at[slot, half(h)], fown.at[slot, half(h)], fsend.at[4 + h], frecv.at[4 + h], peer(d))

    def m_copy(d):
        return copy(mass_ref, massg.at[r], msend.at[d - 1], mrecv.at[d - 1], peer(d))

    def m_arrived(d):
        return copy(mass_ref, massg.at[source(d)], msend.at[d - 1], mrecv.at[d - 1], peer(d))

    def n_copy(d):
        src = f_ref if d == 0 else fown.at[source(d)]
        return copy(src, fnext.at[source(d)], nsend.at[d], nrecv.at[d], (t - 1, r))

    order = (1, 3, 2)
    for d, h in ((1, 0), (3, 1), (1, 1), (3, 0)):
        f_copy(d, h).start()
    for d in order:
        m_copy(d).start()

    @pl.when(t >= 1)
    def _():
        n_copy(0).start()

    fown[r] = f_ref[...]
    massg[r] = mass_ref[...]
    rcur[...] = rhs_ref[...]
    for d, h in ((1, 0), (3, 1)):
        f_arrived(d, h).wait_recv()
        f_on(d, source(d)).start()
    for d, h in ((1, 1), (3, 0)):
        f_arrived(d, h).wait_recv()

        @pl.when(t >= 1)
        def _():
            n_copy(d).start()

    for d in (1, 3):
        f_on(d, source(2)).wait_recv()

    @pl.when(t >= 1)
    def _():
        n_copy(2).start()

    for d in order:
        m_arrived(d).wait_recv()

    row_ids = lax.broadcasted_iota(jnp.int32, (tiles * Q, Q), 0)
    col_ids = lax.broadcasted_iota(jnp.int32, (tiles * Q, Q), 1)

    def own_gram(p, carry):
        full = fown[...].reshape(tiles * Q, tiles * Q)
        pair = fown[pl.ds(2 * p, 2)].reshape(2 * Q, tiles * Q)
        gram = dot(full, pair, 1, 1)
        for e in range(2):
            c = 2 * p + e
            block = gram[:, e * Q : (e + 1) * Q]
            lg[0, c] = -block
            dg[0, c] = block + jnp.where(row_ids == col_ids + c * Q, massg[c], 0.0)
        return carry

    lax.fori_loop(0, tiles // 2, own_gram, 0)

    @pl.when(t + 1 < blocks)
    def _():
        for d in (0,) + order:
            n_copy(d).wait_recv()

        def next_gram(p, carry):
            full = fnext[...].reshape(tiles * Q, tiles * Q)
            pair = fnext[pl.ds(2 * p, 2)].reshape(2 * Q, tiles * Q)
            gram = dot(full, pair, 1, 1)
            for e in range(2):
                c = 2 * p + e
                block = gram[:, e * Q : (e + 1) * Q]
                ug[0, c] = -block
                dg[0, c] = dg[0, c] + block
            return carry

        lax.fori_loop(0, tiles // 2, next_gram, 0)

    for d in (1, 3):
        for h in range(2):
            f_copy(d, h).wait_send()
        f_on(d, source(d)).wait_send()
    for d in order:
        m_copy(d).wait_send()

    @pl.when(t >= 1)
    def _():
        for d in (0,) + order:
            n_copy(d).wait_send()

    def along(i, s, k, c=None):
        device = (t + s, r) if k % 2 == 0 else (t - s, r)
        if k < 2:
            rows = pl.ds(c * Q, Q)
            src, dst, sem = staged.at[i, k, rows], dr.at[i, k, rows], 4 * k + c
        elif k < 4:
            src, dst, sem = pairs.at[i, k - 2, c], (lg if k == 2 else ug).at[i + 1, lax.rem(r + c, tiles)], 6 + 2 * k + c
        else:
            src, dst, sem = staged.at[i, k - 2], rr.at[i, k % 2], 10 + k
        return copy(src, dst, send.at[i, sem], recv.at[i, sem], device)

    def rows_across(i, c, d, slot):
        rows = pl.ds(c * Q, Q)
        sem = 16 + 3 * c + d - 1
        return copy(dg.at[i + 1, r, rows], dg.at[i + 1, slot, rows], send.at[i, sem], recv.at[i, sem], peer(d))

    def coupling_across(i, k, d):
        buffer = (lg, ug)[k]
        slot = r if d == 1 else lax.rem(r + 1, tiles)
        sem = 28 + 2 * k + (0 if d == 1 else 1)
        return copy(buffer.at[i + 1, slot], buffer.at[i + 1, slot], send.at[i, sem], recv.at[i, sem], peer(d))

    def coupling_arrives(i, k, d):
        buffer = (lg, ug)[k]
        slot = lax.rem(r + (3 if d == 1 else 2), tiles)
        sem = 28 + 2 * k + (0 if d == 1 else 1)
        return copy(buffer.at[i + 1, slot], buffer.at[i + 1, slot], send.at[i, sem], recv.at[i, sem], peer(d))

    def couples(i, s, k):
        return (t >= 2 * s) if k == 0 else (t + 2 * s < blocks)

    def take_rows(i, s, c):
        rows = slice(c * Q, (c + 1) * Q)

        @pl.when(r >= c)
        def _():
            dg[i + 1, r, rows] = dg[i, r, rows]

            @pl.when(t >= s)
            def _():
                along(i, s, 0, c).wait_recv()
                dg[i + 1, r, rows] = dg[i + 1, r, rows] - dr[i, 0, rows]

            @pl.when(t + s < blocks)
            def _():
                along(i, s, 1, c).wait_recv()
                dg[i + 1, r, rows] = dg[i + 1, r, rows] - dr[i, 1, rows]

            for d in order:
                rows_across(i, c, d, r).start()

    def spread_couplings(i, s, k):
        @pl.when(couples(i, s, k))
        def _():
            for c in range(2):
                along(i, s, 2 + k, c).wait_recv()
            for d in (1, 3):
                coupling_across(i, k, d).start()

    def couplings_arrived(i, s, k):
        @pl.when(couples(i, s, k))
        def _():
            for d in (1, 3):
                coupling_arrives(i, k, d).wait_recv()

    def take_rhs(i, s):
        @pl.when(t >= s)
        def _():
            along(i, s, 4).wait_recv()
            rcur[...] = rcur[...] - rr[i, 0]

        @pl.when(t + s < blocks)
        def _():
            along(i, s, 5).wait_recv()
            rcur[...] = rcur[...] - rr[i, 1]

    def under(values):
        half = tiles // 2
        cut = half * Q
        upper_half = dot(side([a[c, :cut, :] for c in range(half)]), values[:cut])
        lower_half = dot(side([a[c, cut:, :] for c in range(tiles)]), values)
        return jnp.concatenate([upper_half, lower_half], axis=0)

    def whiten(src, i, base, p):
        first, second = lax.rem(r + 2 * p, tiles), lax.rem(r + 2 * p + 1, tiles)
        both = under(side([src[i, first], src[i, second]]))
        w[base + first] = both[:, :Q]
        w[base + second] = both[:, Q:]

    def level(i, s):
        up, down = t + s < blocks, t >= s
        past, reach = i - 1, s // 2

        def before(j):
            @pl.when(i > 0)
            def _():
                @pl.when(j == 0)
                def _():
                    take_rows(past, reach, 0)
                    take_rows(past, reach, 1)

                for d in order:
                    for c in range(tiles):

                        @pl.when((j == c) & (source(d) >= c))
                        def _():
                            rows_across(past, c, d, source(d)).wait_recv()

        def after(j):
            @pl.when(i > 0)
            def _():
                @pl.when(j == 0)
                def _():
                    take_rows(past, reach, 2)
                    take_rows(past, reach, 3)

                for k in range(2):

                    @pl.when(j == SPREAD[k])
                    def _():
                        spread_couplings(past, reach, k)

        factorize(dg.at[i], a, upper, before, after)

        @pl.when(up)
        def _():
            whiten(ug, i, tiles, 0)

        @pl.when(down)
        def _():
            whiten(lg, i, 0, 0)

        @pl.when(i > 0)
        def _():
            take_rhs(past, reach)

        w[2 * tiles] = under(rcur[...])

        @pl.when(i > 0)
        def _():
            couplings_arrived(past, reach, 0)

        @pl.when(down)
        def _():
            whiten(lg, i, 0, 1)
            earlier = side([w[c] for c in range(tiles)])
            terms = dot(earlier, side([w[r], w[2 * tiles]]), 0, 0)
            staged[i, 1] = terms[:, :Q]
            staged[i, 3] = terms[:, Q:]
            for c in range(tiles):

                @pl.when(r >= c)
                def _():
                    along(i, s, 1, c).start()


        @pl.when(i > 0)
        def _():
            couplings_arrived(past, reach, 1)

        @pl.when(up)
        def _():
            whiten(ug, i, tiles, 1)
            later = side([w[tiles + c] for c in range(tiles)])
            terms = dot(later, side([w[tiles + r], w[2 * tiles]]), 0, 0)
            staged[i, 0] = terms[:, :Q]
            staged[i, 2] = terms[:, Q:]
            for c in range(tiles):

                @pl.when(r >= c)
                def _():
                    along(i, s, 0, c).start()


        @pl.when(up & down)
        def _():
            second = lax.rem(r + 1, tiles)
            later = side([w[tiles + c] for c in range(tiles)])
            product = -dot(later, side([w[r], w[second]]), 0, 0)
            for c in range(2):
                pairs[i, 0, c] = product[:, c * Q : (c + 1) * Q]
                along(i, s, 2, c).start()
            earlier = side([w[c] for c in range(tiles)])
            product = -dot(earlier, side([w[tiles + r], w[tiles + second]]), 0, 0)
            for c in range(2):
                pairs[i, 1, c] = product[:, c * Q : (c + 1) * Q]
                along(i, s, 3, c).start()

        @pl.when(up)
        def _():
            along(i, s, 4).start()

        @pl.when(down)
        def _():
            along(i, s, 5).start()

        return s * 2

    lax.fori_loop(0, levels + 1, level, 1)
    out_ref[...] = dot(side([a[c] for c in range(tiles)]), w[2 * tiles], 0, 0)

    def drain(i, s):
        up, down = t + s < blocks, t >= s

        @pl.when(up)
        def _():
            along(i, s, 4).wait_send()
            for c in range(tiles):

                @pl.when(r >= c)
                def _():
                    along(i, s, 0, c).wait_send()


        @pl.when(down)
        def _():
            along(i, s, 5).wait_send()
            for c in range(tiles):

                @pl.when(r >= c)
                def _():
                    along(i, s, 1, c).wait_send()


        @pl.when(up & down)
        def _():
            for c in range(2):
                along(i, s, 2, c).wait_send()
                along(i, s, 3, c).wait_send()

        for c in range(tiles):

            @pl.when(r >= c)
            def _():
                for d in order:
                    rows_across(i, c, d, r).wait_send()

        for k in range(2):

            @pl.when(couples(i, s, k))
            def _():
                for d in (1, 3):
                    coupling_across(i, k, d).wait_send()

        return s * 2

    lax.fori_loop(0, levels, drain, 1)


def local(edge_factor, mass, rhs):
    blocks = lax.axis_size("tm")
    tiles = lax.axis_size("row")
    levels = (blocks - 1).bit_length()
    quarter, nodes = edge_factor.shape[1:]
    f32 = jnp.float32
    vmem = pl.BlockSpec(memory_space=pltpu.VMEM)
    dma = pltpu.SemaphoreType.DMA
    column = (nodes, quarter)
    mass_rows = jnp.broadcast_to(mass, (1, quarter))
    result = pl.pallas_call(
        functools.partial(kernel, blocks, levels),
        out_shape=jax.ShapeDtypeStruct(column, f32),
        in_specs=[vmem] * 3,
        out_specs=vmem,
        scratch_shapes=[
            pltpu.VMEM((tiles,) + column, f32),
            pltpu.VMEM((tiles,) + column, f32),
            pltpu.VMEM((2 * tiles + 1,) + column, f32),
            pltpu.VMEM(column, f32),
            pltpu.VMEM((tiles, quarter, nodes), f32),
            pltpu.VMEM((tiles, quarter, nodes), f32),
            pltpu.VMEM((tiles, 1, quarter), f32),
            pltpu.VMEM((levels + 1, tiles) + column, f32),
            pltpu.VMEM((levels + 1, tiles) + column, f32),
            pltpu.VMEM((levels + 1, tiles) + column, f32),
            pltpu.VMEM((levels, 2) + column, f32),
            pltpu.VMEM((levels, 2) + column, f32),
            pltpu.VMEM((levels, 4) + column, f32),
            pltpu.VMEM((levels, 2, 2) + column, f32),
            dma((6,)), dma((6,)), dma((4,)), dma((4,)), dma((3,)), dma((3,)),
            dma((levels, 32)), dma((levels, 32)),
        ],
        compiler_params=pltpu.CompilerParams(
            collective_id=0, has_side_effects=True, vmem_limit_bytes=63 * 1024 * 1024
        ),
    )(edge_factor[0], mass_rows, rhs[0])
    return result[None]


def solution(mesh):
    placed = (P("tm", "row", None), P("tm", "row"), P("tm", None, "row"))
    return jax.shard_map(
        local, mesh=mesh, in_specs=placed, out_specs=P("tm", None, "row"), check_vma=False
    )
```

```python
import functools

import jax
import jax.numpy as jnp
from jax import lax
from jax.experimental import pallas as pl
from jax.experimental.pallas import tpu as pltpu
from jax.sharding import PartitionSpec as P

MESH = pl.DeviceIdType.MESH
EXACT = lax.Precision.HIGHEST
Q = 128
SPREAD = (1, 2)
G = 8


def dot(a, b, ca=1, cb=0):
    return lax.dot_general(
        a, b, (((ca,), (cb,)), ((), ())), precision=EXACT, preferred_element_type=jnp.float32
    )


def lanes(v, k):
    return jnp.broadcast_to(v[:, k : k + 1], v.shape)


def subs(v, k):
    return jnp.broadcast_to(v[k : k + 1, :], v.shape)


def eliminate(rows, base):
    lane = lax.broadcasted_iota(jnp.int32, (G, Q), 1)
    sub = lax.broadcasted_iota(jnp.int32, (G, Q), 0)
    rows = list(rows)
    count = len(rows)
    out = []
    cols = [lanes(rows[0], base + k) for k in range(G)]
    for g in range(count):
        c0 = base + G * g
        inside = (lane >= c0) & (lane < c0 + G)
        more = g + 1 < count
        if more:
            near = [lanes(rows[g + 1], c0 + k) for k in range(G)]
            after = [lanes(rows[g + 1], c0 + G + k) for k in range(G)]
            w = jnp.where(inside, 0.0, rows[g + 1])
        v = jnp.where(inside, jnp.where(lane == sub + c0, 1.0, 0.0), rows[g])
        inv, upper = [], {}
        scale = jnp.ones((G, Q), jnp.float32)
        for k in range(G):
            pivot = subs(cols[k], k)
            inv.append(1.0 / pivot)
            scale = jnp.where(sub == k, lax.rsqrt(pivot), scale)
            for k2 in range(k + 1, G):
                upper[k, k2] = subs(cols[k2], k)
            row = subs(v, k)
            if k < G - 1:
                m = jnp.where(sub > k, cols[k] * inv[k], 0.0)
                for k2 in range(k + 1, G):
                    cols[k2] = cols[k2] - m * upper[k, k2]
                v = v - m * row
            if more:
                m = near[k] * inv[k]
                for k2 in range(G):
                    after[k2] = after[k2] - m * subs(near[k], k2)
                for k2 in range(k + 1, G):
                    near[k2] = near[k2] - m * upper[k, k2]
                w = w - m * row
        if more:
            rows[g + 1] = w
            cols = after
        spread = [subs(v, k) for k in range(G)]
        for h in range(g + 2, count):
            below = [lanes(rows[h], c0 + k) for k in range(G)]
            w = jnp.where(inside, 0.0, rows[h])
            for k in range(G):
                m = below[k] * inv[k]
                for k2 in range(k + 1, G):
                    below[k2] = below[k2] - m * upper[k, k2]
                w = w - m * spread[k]
            rows[h] = w
        out.append(v * scale)
    return out


def inverse_factor(rows):
    lane = lax.broadcasted_iota(jnp.int32, (G, Q), 1)
    sub = lax.broadcasted_iota(jnp.int32, (G, Q), 0)
    half, middle = len(rows) // 2, Q // 2
    top = eliminate(rows[:half], 0)
    kept = [jnp.where((lane <= sub + G * g) | (lane >= middle), top[g], 0.0) for g in range(half)]
    stacked = jnp.concatenate(kept, axis=0)
    update = dot(stacked, stacked, 0, 0)
    rest = [jnp.where(lane < middle, 0.0, rows[h]) - update[G * h : G * h + G] for h in range(half, 2 * half)]
    both = top + eliminate(rest, middle)
    return [jnp.where(lane <= sub + G * g, both[g], 0.0) for g in range(2 * half)]


def side(blocks):
    return jnp.concatenate(blocks, axis=1)


def factorize(diag, inverse, upper, before, after):
    tiles = diag.shape[0]

    def step(j, carry):
        here = pl.ds(pl.multiple_of(j * Q, Q), Q)
        before(j)
        for c in range(tiles):
            inverse[c, here, :] = jnp.where(c < j, 0.0, diag[c, here, :])
        for above in range(1, tiles):

            @pl.when(j == above)
            def _():
                rows = slice(0, above * Q)
                known = [(inverse if c < above else upper)[c, rows, :] for c in range(tiles)]
                update = dot(upper[above, rows, :], side(known), 0, 0)
                for c in range(tiles):
                    inverse[c, here, :] = inverse[c, here, :] - update[:, c * Q : (c + 1) * Q]

        rows = [inverse[j, pl.ds(pl.multiple_of(j * Q + G * h, G), G), :] for h in range(Q // G)]
        top = jnp.concatenate(inverse_factor(rows), axis=0)
        across = dot(top, side([inverse[c, here, :] for c in range(tiles)]))
        for c in range(tiles):
            block = across[:, c * Q : (c + 1) * Q]
            upper[c, here, :] = block
            inverse[c, here, :] = jnp.where(c == j, top, jnp.where(c < j, block, 0.0))
        after(j)
        return carry

    lax.fori_loop(0, tiles, step, 0)


def kernel(blocks, levels, f_ref, mass_ref, rhs_ref, out_ref, a, upper, w, rcur, fown, fnext, massg, dg, lg, ug, dr, rr, staged, pairs,
           fsend, frecv, nsend, nrecv, msend, mrecv, send, recv):
    t = lax.axis_index("tm")
    r = lax.axis_index("row")
    tiles = a.shape[0]

    def peer(d):
        return (t, lax.rem(r + d, tiles))

    def source(d):
        return lax.rem(r + tiles - d, tiles)

    def copy(src, dst, ssem, rsem, device):
        return pltpu.make_async_remote_copy(
            src_ref=src, dst_ref=dst, send_sem=ssem, recv_sem=rsem, device_id=device, device_id_type=MESH
        )

    barrier = pltpu.get_barrier_semaphore()
    expected = tiles - 1
    for d in range(1, tiles):
        pl.semaphore_signal(barrier, inc=1, device_id=peer(d), device_id_type=MESH)
    for level in range(levels):
        s = 2**level
        up, down = t + s < blocks, t >= s

        @pl.when(up)
        def _():
            pl.semaphore_signal(barrier, inc=1, device_id=(t + s, r), device_id_type=MESH)

        @pl.when(down)
        def _():
            pl.semaphore_signal(barrier, inc=1, device_id=(t - s, r), device_id_type=MESH)

        expected = expected + up.astype(jnp.int32) + down.astype(jnp.int32)
    pl.semaphore_wait(barrier, expected)

    def half(h):
        return pl.ds(h * (Q // 2), Q // 2)

    def f_copy(d, h):
        sem = d - 1 + h
        return copy(f_ref.at[half(h)], fown.at[r, half(h)], fsend.at[sem], frecv.at[sem], peer(d))

    def f_arrived(d, h):
        sem = d - 1 + h
        return copy(f_ref.at[half(h)], fown.at[source(d), half(h)], fsend.at[sem], frecv.at[sem], peer(d))

    def f_on(d, slot):
        h = 0 if d == 1 else 1
        return copy(fown.at[slot, half(h)], fown.at[slot, half(h)], fsend.at[4 + h], frecv.at[4 + h], peer(d))

    def m_copy(d):
        return copy(mass_ref, massg.at[r], msend.at[d - 1], mrecv.at[d - 1], peer(d))

    def m_arrived(d):
        return copy(mass_ref, massg.at[source(d)], msend.at[d - 1], mrecv.at[d - 1], peer(d))

    def n_copy(d):
        src = f_ref if d == 0 else fown.at[source(d)]
        return copy(src, fnext.at[source(d)], nsend.at[d], nrecv.at[d], (t - 1, r))

    order = (1, 3, 2)
    for d, h in ((1, 0), (3, 1), (1, 1), (3, 0)):
        f_copy(d, h).start()
    for d in order:
        m_copy(d).start()

    @pl.when(t >= 1)
    def _():
        n_copy(0).start()

    fown[r] = f_ref[...]
    massg[r] = mass_ref[...]
    rcur[...] = rhs_ref[...]
    for d, h in ((1, 0), (3, 1)):
        f_arrived(d, h).wait_recv()
        f_on(d, source(d)).start()
    for d, h in ((1, 1), (3, 0)):
        f_arrived(d, h).wait_recv()

        @pl.when(t >= 1)
        def _():
            n_copy(d).start()

    for d in (1, 3):
        f_on(d, source(2)).wait_recv()

    @pl.when(t >= 1)
    def _():
        n_copy(2).start()

    for d in order:
        m_arrived(d).wait_recv()

    row_ids = lax.broadcasted_iota(jnp.int32, (tiles * Q, Q), 0)
    col_ids = lax.broadcasted_iota(jnp.int32, (tiles * Q, Q), 1)

    def own_gram(p, carry):
        full = fown[...].reshape(tiles * Q, tiles * Q)
        pair = fown[pl.ds(2 * p, 2)].reshape(2 * Q, tiles * Q)
        gram = dot(full, pair, 1, 1)
        for e in range(2):
            c = 2 * p + e
            block = gram[:, e * Q : (e + 1) * Q]
            lg[0, c] = -block
            dg[0, c] = block + jnp.where(row_ids == col_ids + c * Q, massg[c], 0.0)
        return carry

    lax.fori_loop(0, tiles // 2, own_gram, 0)

    @pl.when(t + 1 < blocks)
    def _():
        for d in (0,) + order:
            n_copy(d).wait_recv()

        def next_gram(p, carry):
            full = fnext[...].reshape(tiles * Q, tiles * Q)
            pair = fnext[pl.ds(2 * p, 2)].reshape(2 * Q, tiles * Q)
            gram = dot(full, pair, 1, 1)
            for e in range(2):
                c = 2 * p + e
                block = gram[:, e * Q : (e + 1) * Q]
                ug[0, c] = -block
                dg[0, c] = dg[0, c] + block
            return carry

        lax.fori_loop(0, tiles // 2, next_gram, 0)

    for d in (1, 3):
        for h in range(2):
            f_copy(d, h).wait_send()
        f_on(d, source(d)).wait_send()
    for d in order:
        m_copy(d).wait_send()

    @pl.when(t >= 1)
    def _():
        for d in (0,) + order:
            n_copy(d).wait_send()

    def along(i, s, k, c=None):
        device = (t + s, r) if k % 2 == 0 else (t - s, r)
        if k < 2:
            rows = pl.ds(c * Q, Q)
            src, dst, sem = staged.at[i, k, rows], dr.at[i, k, rows], 4 * k + c
        elif k < 4:
            src, dst, sem = pairs.at[i, k - 2, c], (lg if k == 2 else ug).at[i + 1, lax.rem(r + c, tiles)], 6 + 2 * k + c
        else:
            src, dst, sem = staged.at[i, k - 2], rr.at[i, k % 2], 10 + k
        return copy(src, dst, send.at[i, sem], recv.at[i, sem], device)

    def rows_across(i, c, d, slot):
        rows = pl.ds(c * Q, Q)
        sem = 16 + 3 * c + d - 1
        return copy(dg.at[i + 1, r, rows], dg.at[i + 1, slot, rows], send.at[i, sem], recv.at[i, sem], peer(d))

    def coupling_across(i, k, d):
        buffer = (lg, ug)[k]
        slot = r if d == 1 else lax.rem(r + 1, tiles)
        sem = 28 + 2 * k + (0 if d == 1 else 1)
        return copy(buffer.at[i + 1, slot], buffer.at[i + 1, slot], send.at[i, sem], recv.at[i, sem], peer(d))

    def coupling_arrives(i, k, d):
        buffer = (lg, ug)[k]
        slot = lax.rem(r + (3 if d == 1 else 2), tiles)
        sem = 28 + 2 * k + (0 if d == 1 else 1)
        return copy(buffer.at[i + 1, slot], buffer.at[i + 1, slot], send.at[i, sem], recv.at[i, sem], peer(d))

    def couples(i, s, k):
        return (t >= 2 * s) if k == 0 else (t + 2 * s < blocks)

    def take_rows(i, s, c):
        rows = slice(c * Q, (c + 1) * Q)

        @pl.when(r >= c)
        def _():
            dg[i + 1, r, rows] = dg[i, r, rows]

            @pl.when(t >= s)
            def _():
                along(i, s, 0, c).wait_recv()
                dg[i + 1, r, rows] = dg[i + 1, r, rows] - dr[i, 0, rows]

            @pl.when(t + s < blocks)
            def _():
                along(i, s, 1, c).wait_recv()
                dg[i + 1, r, rows] = dg[i + 1, r, rows] - dr[i, 1, rows]

            for d in order:
                rows_across(i, c, d, r).start()

    def spread_couplings(i, s, k):
        @pl.when(couples(i, s, k))
        def _():
            for c in range(2):
                along(i, s, 2 + k, c).wait_recv()
            for d in (1, 3):
                coupling_across(i, k, d).start()

    def couplings_arrived(i, s, k):
        @pl.when(couples(i, s, k))
        def _():
            for d in (1, 3):
                coupling_arrives(i, k, d).wait_recv()

    def take_rhs(i, s):
        @pl.when(t >= s)
        def _():
            along(i, s, 4).wait_recv()
            rcur[...] = rcur[...] - rr[i, 0]

        @pl.when(t + s < blocks)
        def _():
            along(i, s, 5).wait_recv()
            rcur[...] = rcur[...] - rr[i, 1]

    def under(values):
        half = tiles // 2
        cut = half * Q
        upper_half = dot(side([a[c, :cut, :] for c in range(half)]), values[:cut])
        lower_half = dot(side([a[c, cut:, :] for c in range(tiles)]), values)
        return jnp.concatenate([upper_half, lower_half], axis=0)

    def whiten(src, i, base, p):
        first, second = lax.rem(r + 2 * p, tiles), lax.rem(r + 2 * p + 1, tiles)
        both = under(side([src[i, first], src[i, second]]))
        w[base + first] = both[:, :Q]
        w[base + second] = both[:, Q:]

    def level(i, s):
        up, down = t + s < blocks, t >= s
        past, reach = i - 1, s // 2

        def before(j):
            @pl.when(i > 0)
            def _():
                @pl.when(j == 0)
                def _():
                    take_rows(past, reach, 0)
                    take_rows(past, reach, 1)

                for d in order:
                    for c in range(tiles):

                        @pl.when((j == c) & (source(d) >= c))
                        def _():
                            rows_across(past, c, d, source(d)).wait_recv()

        def after(j):
            @pl.when(i > 0)
            def _():
                @pl.when(j == 0)
                def _():
                    take_rows(past, reach, 2)
                    take_rows(past, reach, 3)

                for k in range(2):

                    @pl.when(j == SPREAD[k])
                    def _():
                        spread_couplings(past, reach, k)

        factorize(dg.at[i], a, upper, before, after)

        @pl.when(up)
        def _():
            whiten(ug, i, tiles, 0)

        @pl.when(down)
        def _():
            whiten(lg, i, 0, 0)

        @pl.when(i > 0)
        def _():
            couplings_arrived(past, reach, 0)

        @pl.when(down)
        def _():
            whiten(lg, i, 0, 1)

        @pl.when(i > 0)
        def _():
            take_rhs(past, reach)

        w[2 * tiles] = under(rcur[...])

        @pl.when(down)
        def _():
            earlier = side([w[c] for c in range(tiles)])
            terms = dot(earlier, side([w[r], w[2 * tiles]]), 0, 0)
            staged[i, 1] = terms[:, :Q]
            staged[i, 3] = terms[:, Q:]
            for c in range(tiles):

                @pl.when(r >= c)
                def _():
                    along(i, s, 1, c).start()


        @pl.when(i > 0)
        def _():
            couplings_arrived(past, reach, 1)

        @pl.when(up)
        def _():
            whiten(ug, i, tiles, 1)
            later = side([w[tiles + c] for c in range(tiles)])
            terms = dot(later, side([w[tiles + r], w[2 * tiles]]), 0, 0)
            staged[i, 0] = terms[:, :Q]
            staged[i, 2] = terms[:, Q:]
            for c in range(tiles):

                @pl.when(r >= c)
                def _():
                    along(i, s, 0, c).start()


        @pl.when(up & down)
        def _():
            second = lax.rem(r + 1, tiles)
            later = side([w[tiles + c] for c in range(tiles)])
            product = -dot(later, side([w[r], w[second]]), 0, 0)
            for c in range(2):
                pairs[i, 0, c] = product[:, c * Q : (c + 1) * Q]
                along(i, s, 2, c).start()
            earlier = side([w[c] for c in range(tiles)])
            product = -dot(earlier, side([w[tiles + r], w[tiles + second]]), 0, 0)
            for c in range(2):
                pairs[i, 1, c] = product[:, c * Q : (c + 1) * Q]
                along(i, s, 3, c).start()

        @pl.when(up)
        def _():
            along(i, s, 4).start()

        @pl.when(down)
        def _():
            along(i, s, 5).start()

        return s * 2

    lax.fori_loop(0, levels + 1, level, 1)
    out_ref[...] = dot(side([a[c] for c in range(tiles)]), w[2 * tiles], 0, 0)

    def drain(i, s):
        up, down = t + s < blocks, t >= s

        @pl.when(up)
        def _():
            along(i, s, 4).wait_send()
            for c in range(tiles):

                @pl.when(r >= c)
                def _():
                    along(i, s, 0, c).wait_send()


        @pl.when(down)
        def _():
            along(i, s, 5).wait_send()
            for c in range(tiles):

                @pl.when(r >= c)
                def _():
                    along(i, s, 1, c).wait_send()


        @pl.when(up & down)
        def _():
            for c in range(2):
                along(i, s, 2, c).wait_send()
                along(i, s, 3, c).wait_send()

        for c in range(tiles):

            @pl.when(r >= c)
            def _():
                for d in order:
                    rows_across(i, c, d, r).wait_send()

        for k in range(2):

            @pl.when(couples(i, s, k))
            def _():
                for d in (1, 3):
                    coupling_across(i, k, d).wait_send()

        return s * 2

    lax.fori_loop(0, levels, drain, 1)


def local(edge_factor, mass, rhs):
    blocks = lax.axis_size("tm")
    tiles = lax.axis_size("row")
    levels = (blocks - 1).bit_length()
    quarter, nodes = edge_factor.shape[1:]
    f32 = jnp.float32
    vmem = pl.BlockSpec(memory_space=pltpu.VMEM)
    dma = pltpu.SemaphoreType.DMA
    column = (nodes, quarter)
    mass_rows = jnp.broadcast_to(mass, (1, quarter))
    result = pl.pallas_call(
        functools.partial(kernel, blocks, levels),
        out_shape=jax.ShapeDtypeStruct(column, f32),
        in_specs=[vmem] * 3,
        out_specs=vmem,
        scratch_shapes=[
            pltpu.VMEM((tiles,) + column, f32),
            pltpu.VMEM((tiles,) + column, f32),
            pltpu.VMEM((2 * tiles + 1,) + column, f32),
            pltpu.VMEM(column, f32),
            pltpu.VMEM((tiles, quarter, nodes), f32),
            pltpu.VMEM((tiles, quarter, nodes), f32),
            pltpu.VMEM((tiles, 1, quarter), f32),
            pltpu.VMEM((levels + 1, tiles) + column, f32),
            pltpu.VMEM((levels + 1, tiles) + column, f32),
            pltpu.VMEM((levels + 1, tiles) + column, f32),
            pltpu.VMEM((levels, 2) + column, f32),
            pltpu.VMEM((levels, 2) + column, f32),
            pltpu.VMEM((levels, 4) + column, f32),
            pltpu.VMEM((levels, 2, 2) + column, f32),
            dma((6,)), dma((6,)), dma((4,)), dma((4,)), dma((3,)), dma((3,)),
            dma((levels, 32)), dma((levels, 32)),
        ],
        compiler_params=pltpu.CompilerParams(
            collective_id=0, has_side_effects=True, vmem_limit_bytes=63 * 1024 * 1024
        ),
    )(edge_factor[0], mass_rows, rhs[0])
    return result[None]


def solution(mesh):
    placed = (P("tm", "row", None), P("tm", "row"), P("tm", None, "row"))
    return jax.shard_map(
        local, mesh=mesh, in_specs=placed, out_specs=P("tm", None, "row"), check_vma=False
    )
```

```python
import functools

import jax
import jax.numpy as jnp
from jax import lax
from jax.experimental import pallas as pl
from jax.experimental.pallas import tpu as pltpu
from jax.sharding import PartitionSpec as P

MESH = pl.DeviceIdType.MESH
EXACT = lax.Precision.HIGHEST
Q = 128
SPREAD = (1, 2)
G = 8


def dot(a, b, ca=1, cb=0):
    return lax.dot_general(
        a, b, (((ca,), (cb,)), ((), ())), precision=EXACT, preferred_element_type=jnp.float32
    )


def lanes(v, k):
    return jnp.broadcast_to(v[:, k : k + 1], v.shape)


def subs(v, k):
    return jnp.broadcast_to(v[k : k + 1, :], v.shape)


def eliminate(rows, base):
    lane = lax.broadcasted_iota(jnp.int32, (G, Q), 1)
    sub = lax.broadcasted_iota(jnp.int32, (G, Q), 0)
    rows = list(rows)
    count = len(rows)
    out = []
    cols = [lanes(rows[0], base + k) for k in range(G)]
    for g in range(count):
        c0 = base + G * g
        inside = (lane >= c0) & (lane < c0 + G)
        more = g + 1 < count
        if more:
            near = [lanes(rows[g + 1], c0 + k) for k in range(G)]
            after = [lanes(rows[g + 1], c0 + G + k) for k in range(G)]
            w = jnp.where(inside, 0.0, rows[g + 1])
        v = jnp.where(inside, jnp.where(lane == sub + c0, 1.0, 0.0), rows[g])
        inv, upper = [], {}
        scale = jnp.ones((G, Q), jnp.float32)
        for k in range(G):
            pivot = subs(cols[k], k)
            inv.append(1.0 / pivot)
            scale = jnp.where(sub == k, lax.rsqrt(pivot), scale)
            for k2 in range(k + 1, G):
                upper[k, k2] = subs(cols[k2], k)
            row = subs(v, k)
            if k < G - 1:
                m = jnp.where(sub > k, cols[k] * inv[k], 0.0)
                for k2 in range(k + 1, G):
                    cols[k2] = cols[k2] - m * upper[k, k2]
                v = v - m * row
            if more:
                m = near[k] * inv[k]
                for k2 in range(G):
                    after[k2] = after[k2] - m * subs(near[k], k2)
                for k2 in range(k + 1, G):
                    near[k2] = near[k2] - m * upper[k, k2]
                w = w - m * row
        if more:
            rows[g + 1] = w
            cols = after
        spread = [subs(v, k) for k in range(G)]
        for h in range(g + 2, count):
            below = [lanes(rows[h], c0 + k) for k in range(G)]
            w = jnp.where(inside, 0.0, rows[h])
            for k in range(G):
                m = below[k] * inv[k]
                for k2 in range(k + 1, G):
                    below[k2] = below[k2] - m * upper[k, k2]
                w = w - m * spread[k]
            rows[h] = w
        out.append(v * scale)
    return out


def inverse_factor(rows):
    lane = lax.broadcasted_iota(jnp.int32, (G, Q), 1)
    sub = lax.broadcasted_iota(jnp.int32, (G, Q), 0)
    half, middle = len(rows) // 2, Q // 2
    top = eliminate(rows[:half], 0)
    kept = [jnp.where((lane <= sub + G * g) | (lane >= middle), top[g], 0.0) for g in range(half)]
    stacked = jnp.concatenate(kept, axis=0)
    update = dot(stacked, stacked, 0, 0)
    rest = [jnp.where(lane < middle, 0.0, rows[h]) - update[G * h : G * h + G] for h in range(half, 2 * half)]
    both = top + eliminate(rest, middle)
    return [jnp.where(lane <= sub + G * g, both[g], 0.0) for g in range(2 * half)]


def side(blocks):
    return jnp.concatenate(blocks, axis=1)


def factorize(diag, inverse, upper, before, after):
    tiles = diag.shape[0]

    def step(j, carry):
        here = pl.ds(pl.multiple_of(j * Q, Q), Q)
        before(j)
        for c in range(tiles):
            inverse[c, here, :] = jnp.where(c < j, 0.0, diag[c, here, :])
        for above in range(1, tiles):

            @pl.when(j == above)
            def _():
                rows = slice(0, above * Q)
                known = [(inverse if c < above else upper)[c, rows, :] for c in range(tiles)]
                update = dot(upper[above, rows, :], side(known), 0, 0)
                for c in range(tiles):
                    inverse[c, here, :] = inverse[c, here, :] - update[:, c * Q : (c + 1) * Q]

        rows = [inverse[j, pl.ds(pl.multiple_of(j * Q + G * h, G), G), :] for h in range(Q // G)]
        top = jnp.concatenate(inverse_factor(rows), axis=0)
        across = dot(top, side([inverse[c, here, :] for c in range(tiles)]))
        for c in range(tiles):
            block = across[:, c * Q : (c + 1) * Q]
            upper[c, here, :] = block
            inverse[c, here, :] = jnp.where(c == j, top, jnp.where(c < j, block, 0.0))
        after(j)
        return carry

    lax.fori_loop(0, tiles, step, 0)


def kernel(blocks, levels, f_ref, mass_ref, rhs_ref, out_ref, a, upper, w, rcur, fown, fnext, massg, dg, lg, ug, dr, rr, staged, pairs,
           fsend, frecv, nsend, nrecv, msend, mrecv, send, recv):
    t = lax.axis_index("tm")
    r = lax.axis_index("row")
    tiles = a.shape[0]

    def peer(d):
        return (t, lax.rem(r + d, tiles))

    def source(d):
        return lax.rem(r + tiles - d, tiles)

    def copy(src, dst, ssem, rsem, device):
        return pltpu.make_async_remote_copy(
            src_ref=src, dst_ref=dst, send_sem=ssem, recv_sem=rsem, device_id=device, device_id_type=MESH
        )

    barrier = pltpu.get_barrier_semaphore()
    expected = tiles - 1
    for d in range(1, tiles):
        pl.semaphore_signal(barrier, inc=1, device_id=peer(d), device_id_type=MESH)
    for level in range(levels):
        s = 2**level
        up, down = t + s < blocks, t >= s

        @pl.when(up)
        def _():
            pl.semaphore_signal(barrier, inc=1, device_id=(t + s, r), device_id_type=MESH)

        @pl.when(down)
        def _():
            pl.semaphore_signal(barrier, inc=1, device_id=(t - s, r), device_id_type=MESH)

        expected = expected + up.astype(jnp.int32) + down.astype(jnp.int32)
    pl.semaphore_wait(barrier, expected)

    def half(h):
        return pl.ds(h * (Q // 2), Q // 2)

    def f_copy(d, h):
        sem = d - 1 + h
        return copy(f_ref.at[half(h)], fown.at[r, half(h)], fsend.at[sem], frecv.at[sem], peer(d))

    def f_arrived(d, h):
        sem = d - 1 + h
        return copy(f_ref.at[half(h)], fown.at[source(d), half(h)], fsend.at[sem], frecv.at[sem], peer(d))

    def f_on(d, slot):
        h = 0 if d == 1 else 1
        return copy(fown.at[slot, half(h)], fown.at[slot, half(h)], fsend.at[4 + h], frecv.at[4 + h], peer(d))

    def m_copy(d):
        return copy(mass_ref, massg.at[r], msend.at[d - 1], mrecv.at[d - 1], peer(d))

    def m_arrived(d):
        return copy(mass_ref, massg.at[source(d)], msend.at[d - 1], mrecv.at[d - 1], peer(d))

    def n_copy(d):
        src = f_ref if d == 0 else fown.at[source(d)]
        return copy(src, fnext.at[source(d)], nsend.at[d], nrecv.at[d], (t - 1, r))

    order = (1, 3, 2)
    for d, h in ((1, 0), (3, 1), (1, 1), (3, 0)):
        f_copy(d, h).start()
    for d in order:
        m_copy(d).start()

    @pl.when(t >= 1)
    def _():
        n_copy(0).start()

    fown[r] = f_ref[...]
    massg[r] = mass_ref[...]
    rcur[...] = rhs_ref[...]
    for d, h in ((1, 0), (3, 1)):
        f_arrived(d, h).wait_recv()
        f_on(d, source(d)).start()
    for d, h in ((1, 1), (3, 0)):
        f_arrived(d, h).wait_recv()

        @pl.when(t >= 1)
        def _():
            n_copy(d).start()

    for d in (1, 3):
        f_on(d, source(2)).wait_recv()

    @pl.when(t >= 1)
    def _():
        n_copy(2).start()

    for d in order:
        m_arrived(d).wait_recv()

    row_ids = lax.broadcasted_iota(jnp.int32, (tiles * Q, Q), 0)
    col_ids = lax.broadcasted_iota(jnp.int32, (tiles * Q, Q), 1)

    def own_gram(p, carry):
        full = fown[...].reshape(tiles * Q, tiles * Q)
        pair = fown[pl.ds(2 * p, 2)].reshape(2 * Q, tiles * Q)
        gram = dot(full, pair, 1, 1)
        for e in range(2):
            c = 2 * p + e
            block = gram[:, e * Q : (e + 1) * Q]
            lg[0, c] = -block
            dg[0, c] = block + jnp.where(row_ids == col_ids + c * Q, massg[c], 0.0)
        return carry

    lax.fori_loop(0, tiles // 2, own_gram, 0)

    @pl.when(t + 1 < blocks)
    def _():
        for d in (0,) + order:
            n_copy(d).wait_recv()

        def next_gram(p, carry):
            full = fnext[...].reshape(tiles * Q, tiles * Q)
            pair = fnext[pl.ds(2 * p, 2)].reshape(2 * Q, tiles * Q)
            gram = dot(full, pair, 1, 1)
            for e in range(2):
                c = 2 * p + e
                block = gram[:, e * Q : (e + 1) * Q]
                ug[0, c] = -block
                dg[0, c] = dg[0, c] + block
            return carry

        lax.fori_loop(0, tiles // 2, next_gram, 0)

    for d in (1, 3):
        for h in range(2):
            f_copy(d, h).wait_send()
        f_on(d, source(d)).wait_send()
    for d in order:
        m_copy(d).wait_send()

    @pl.when(t >= 1)
    def _():
        for d in (0,) + order:
            n_copy(d).wait_send()

    def along(i, s, k, c=None):
        device = (t + s, r) if k % 2 == 0 else (t - s, r)
        if k < 2:
            rows = pl.ds(c * Q, Q)
            src, dst, sem = staged.at[i, k, rows], dr.at[i, k, rows], 4 * k + c
        elif k < 4:
            src, dst, sem = pairs.at[i, k - 2, c], (lg if k == 2 else ug).at[i + 1, lax.rem(r + c, tiles)], 6 + 2 * k + c
        else:
            src, dst, sem = staged.at[i, k - 2], rr.at[i, k % 2], 10 + k
        return copy(src, dst, send.at[i, sem], recv.at[i, sem], device)

    def rows_across(i, c, d, slot):
        rows = pl.ds(c * Q, Q)
        sem = 16 + 3 * c + d - 1
        return copy(dg.at[i + 1, r, rows], dg.at[i + 1, slot, rows], send.at[i, sem], recv.at[i, sem], peer(d))

    def coupling_across(i, k, d):
        buffer = (lg, ug)[k]
        slot = r if d == 1 else lax.rem(r + 1, tiles)
        sem = 28 + 2 * k + (0 if d == 1 else 1)
        return copy(buffer.at[i + 1, slot], buffer.at[i + 1, slot], send.at[i, sem], recv.at[i, sem], peer(d))

    def coupling_arrives(i, k, d):
        buffer = (lg, ug)[k]
        slot = lax.rem(r + (3 if d == 1 else 2), tiles)
        sem = 28 + 2 * k + (0 if d == 1 else 1)
        return copy(buffer.at[i + 1, slot], buffer.at[i + 1, slot], send.at[i, sem], recv.at[i, sem], peer(d))

    def couples(i, s, k):
        return (t >= 2 * s) if k == 0 else (t + 2 * s < blocks)

    def take_rows(i, s, c):
        rows = slice(c * Q, (c + 1) * Q)

        @pl.when(r >= c)
        def _():
            dg[i + 1, r, rows] = dg[i, r, rows]

            @pl.when(t >= s)
            def _():
                along(i, s, 0, c).wait_recv()
                dg[i + 1, r, rows] = dg[i + 1, r, rows] - dr[i, 0, rows]

            @pl.when(t + s < blocks)
            def _():
                along(i, s, 1, c).wait_recv()
                dg[i + 1, r, rows] = dg[i + 1, r, rows] - dr[i, 1, rows]

            for d in order:
                rows_across(i, c, d, r).start()

    def spread_couplings(i, s, k):
        @pl.when(couples(i, s, k))
        def _():
            for c in range(2):
                along(i, s, 2 + k, c).wait_recv()
            for d in (1, 3):
                coupling_across(i, k, d).start()

    def couplings_arrived(i, s, k):
        @pl.when(couples(i, s, k))
        def _():
            for d in (1, 3):
                coupling_arrives(i, k, d).wait_recv()

    def take_rhs(i, s):
        @pl.when(t >= s)
        def _():
            along(i, s, 4).wait_recv()
            rcur[...] = rcur[...] - rr[i, 0]

        @pl.when(t + s < blocks)
        def _():
            along(i, s, 5).wait_recv()
            rcur[...] = rcur[...] - rr[i, 1]

    def under(values):
        half = tiles // 2
        cut = half * Q
        upper_half = dot(side([a[c, :cut, :] for c in range(half)]), values[:cut])
        lower_half = dot(side([a[c, cut:, :] for c in range(tiles)]), values)
        return jnp.concatenate([upper_half, lower_half], axis=0)

    def whiten(src, i, base, p):
        first, second = lax.rem(r + 2 * p, tiles), lax.rem(r + 2 * p + 1, tiles)
        both = under(side([src[i, first], src[i, second]]))
        w[base + first] = both[:, :Q]
        w[base + second] = both[:, Q:]

    def level(i, s):
        up, down = t + s < blocks, t >= s
        past, reach = i - 1, s // 2

        def before(j):
            @pl.when(i > 0)
            def _():
                @pl.when(j == 0)
                def _():
                    take_rows(past, reach, 0)
                    take_rows(past, reach, 1)

                for d in order:
                    for c in range(tiles):

                        @pl.when((j == c) & (source(d) >= c))
                        def _():
                            rows_across(past, c, d, source(d)).wait_recv()

        def after(j):
            @pl.when(i > 0)
            def _():
                @pl.when(j == 0)
                def _():
                    take_rows(past, reach, 2)
                    take_rows(past, reach, 3)

                for k in range(2):

                    @pl.when(j == SPREAD[k] - (i == 1).astype(jnp.int32))
                    def _():
                        spread_couplings(past, reach, k)

        factorize(dg.at[i], a, upper, before, after)

        @pl.when(up)
        def _():
            whiten(ug, i, tiles, 0)

        @pl.when(down)
        def _():
            whiten(lg, i, 0, 0)

        @pl.when(i > 0)
        def _():
            couplings_arrived(past, reach, 0)

        @pl.when(down)
        def _():
            whiten(lg, i, 0, 1)

        @pl.when(i > 0)
        def _():
            take_rhs(past, reach)

        w[2 * tiles] = under(rcur[...])

        @pl.when(down)
        def _():
            earlier = side([w[c] for c in range(tiles)])
            terms = dot(earlier, side([w[r], w[2 * tiles]]), 0, 0)
            staged[i, 1] = terms[:, :Q]
            staged[i, 3] = terms[:, Q:]
            for c in range(tiles):

                @pl.when(r >= c)
                def _():
                    along(i, s, 1, c).start()


        @pl.when(i > 0)
        def _():
            couplings_arrived(past, reach, 1)

        @pl.when(up)
        def _():
            whiten(ug, i, tiles, 1)
            later = side([w[tiles + c] for c in range(tiles)])
            terms = dot(later, side([w[tiles + r], w[2 * tiles]]), 0, 0)
            staged[i, 0] = terms[:, :Q]
            staged[i, 2] = terms[:, Q:]
            for c in range(tiles):

                @pl.when(r >= c)
                def _():
                    along(i, s, 0, c).start()


        @pl.when(up & down)
        def _():
            second = lax.rem(r + 1, tiles)
            later = side([w[tiles + c] for c in range(tiles)])
            product = -dot(later, side([w[r], w[second]]), 0, 0)
            for c in range(2):
                pairs[i, 0, c] = product[:, c * Q : (c + 1) * Q]
                along(i, s, 2, c).start()
            earlier = side([w[c] for c in range(tiles)])
            product = -dot(earlier, side([w[tiles + r], w[tiles + second]]), 0, 0)
            for c in range(2):
                pairs[i, 1, c] = product[:, c * Q : (c + 1) * Q]
                along(i, s, 3, c).start()

        @pl.when(up)
        def _():
            along(i, s, 4).start()

        @pl.when(down)
        def _():
            along(i, s, 5).start()

        return s * 2

    lax.fori_loop(0, levels + 1, level, 1)
    out_ref[...] = dot(side([a[c] for c in range(tiles)]), w[2 * tiles], 0, 0)

    def drain(i, s):
        up, down = t + s < blocks, t >= s

        @pl.when(up)
        def _():
            along(i, s, 4).wait_send()
            for c in range(tiles):

                @pl.when(r >= c)
                def _():
                    along(i, s, 0, c).wait_send()


        @pl.when(down)
        def _():
            along(i, s, 5).wait_send()
            for c in range(tiles):

                @pl.when(r >= c)
                def _():
                    along(i, s, 1, c).wait_send()


        @pl.when(up & down)
        def _():
            for c in range(2):
                along(i, s, 2, c).wait_send()
                along(i, s, 3, c).wait_send()

        for c in range(tiles):

            @pl.when(r >= c)
            def _():
                for d in order:
                    rows_across(i, c, d, r).wait_send()

        for k in range(2):

            @pl.when(couples(i, s, k))
            def _():
                for d in (1, 3):
                    coupling_across(i, k, d).wait_send()

        return s * 2

    lax.fori_loop(0, levels, drain, 1)


def local(edge_factor, mass, rhs):
    blocks = lax.axis_size("tm")
    tiles = lax.axis_size("row")
    levels = (blocks - 1).bit_length()
    quarter, nodes = edge_factor.shape[1:]
    f32 = jnp.float32
    vmem = pl.BlockSpec(memory_space=pltpu.VMEM)
    dma = pltpu.SemaphoreType.DMA
    column = (nodes, quarter)
    mass_rows = jnp.broadcast_to(mass, (1, quarter))
    result = pl.pallas_call(
        functools.partial(kernel, blocks, levels),
        out_shape=jax.ShapeDtypeStruct(column, f32),
        in_specs=[vmem] * 3,
        out_specs=vmem,
        scratch_shapes=[
            pltpu.VMEM((tiles,) + column, f32),
            pltpu.VMEM((tiles,) + column, f32),
            pltpu.VMEM((2 * tiles + 1,) + column, f32),
            pltpu.VMEM(column, f32),
            pltpu.VMEM((tiles, quarter, nodes), f32),
            pltpu.VMEM((tiles, quarter, nodes), f32),
            pltpu.VMEM((tiles, 1, quarter), f32),
            pltpu.VMEM((levels + 1, tiles) + column, f32),
            pltpu.VMEM((levels + 1, tiles) + column, f32),
            pltpu.VMEM((levels + 1, tiles) + column, f32),
            pltpu.VMEM((levels, 2) + column, f32),
            pltpu.VMEM((levels, 2) + column, f32),
            pltpu.VMEM((levels, 4) + column, f32),
            pltpu.VMEM((levels, 2, 2) + column, f32),
            dma((6,)), dma((6,)), dma((4,)), dma((4,)), dma((3,)), dma((3,)),
            dma((levels, 32)), dma((levels, 32)),
        ],
        compiler_params=pltpu.CompilerParams(
            collective_id=0, has_side_effects=True, vmem_limit_bytes=63 * 1024 * 1024
        ),
    )(edge_factor[0], mass_rows, rhs[0])
    return result[None]


def solution(mesh):
    placed = (P("tm", "row", None), P("tm", "row"), P("tm", None, "row"))
    return jax.shard_map(
        local, mesh=mesh, in_specs=placed, out_specs=P("tm", None, "row"), check_vma=False
    )
```
